32 devices in a mesh: group: 2 (over x), head: 2 (over core), blk: 8 (over z, y).
Axes of the slice: x: 2, y: 2, z: 4, core: 2. Of those that a mesh axis runs over, the one named last changes fastest.
Arguments:
- patches: bfloat16 [4096, 1024], P(('group', 'head', 'blk')), parts along dimension 0, may hold values from -60 to 60
- ln_gain: float32 [1024], replicated, may hold values from 0.1 to 1.9
- w_qkv: bfloat16 [1024, 3072], replicated, may hold values from -0.21875 to 0.21875
- qk_gains: float32 [2, 1024], replicated, may hold values from 0.5 to 6
- w_out: bfloat16 [1024, 1024], replicated, may hold values from -0.1875 to 0.1875
Outputs:
- attn_out: bfloat16 [4096, 1024], P(('group', 'head', 'blk')), parts along dimension 0
The draws below stay inside these ranges and needn't reach their ends.
There are 2 independent parts, one for each index of `group`. The reference program is written for one: setup_inputs(seed, part) draws one part's arguments, and reference() takes and returns one part's arrays. A program takes and returns all parts, laid end to end along the dimension named above; an argument that names none is the same for every part. Nothing has to cross between parts.
All inputs are finite; a program needn't handle non-finite values.
Results may differ from the reference program's by a relative error of at most 0.025.
Values may be sent and summed in bfloat16 or wider, within the bound.
A program may use at most 128 MiB of HBM per device.

```python
import math
import jax
import jax.numpy as jnp
from jax import lax

D = 1024
H = 16
HD = 64
TOKENS = 2048


def draw_patches(key, part):
    key_base = jax.random.fold_in(key, 11)
    base_rows = jax.random.normal(key_base, (TOKENS, D), jnp.float32)
    drawn = jnp.clip(base_rows, -6.0, 6.0)
    return drawn.astype(jnp.bfloat16)


def draw_w_qkv(key, part):
    scale_factor = D ** (-0.5)
    query_part = jnp.clip(jax.random.normal(jax.random.fold_in(key, 21), (D, D), jnp.float32), -6.0, 6.0) * scale_factor
    key_fresh = jnp.clip(jax.random.normal(jax.random.fold_in(key, 22), (D, D), jnp.float32), -6.0, 6.0) * scale_factor
    value_part = jnp.clip(jax.random.normal(jax.random.fold_in(key, 23), (D, D), jnp.float32), -6.0, 6.0) * scale_factor
    key_part = key_fresh
    return jnp.concatenate([query_part, key_part, value_part], axis=1).astype(jnp.bfloat16)


def draw_qk_gains(key, part):
    drawn = jnp.exp(jax.random.uniform(jax.random.fold_in(key, 33), (2, D), jnp.float32, math.log(0.5), math.log(2.5)))
    return drawn.astype(jnp.float32)


def scatter_about(rng, extent, spread, reach, held_as=jnp.bfloat16):
    return jnp.clip(spread * jax.random.normal(rng, extent, jnp.float32), -reach, reach).astype(held_as)


def setup_inputs(seed: int = 0, part: int = 0) -> dict:
    splits = jax.random.split(jax.random.key(seed), 6)
    part_keys = jax.random.split(jax.random.fold_in(splits[5], part), 6)
    patches = draw_patches(jax.random.fold_in(jax.random.fold_in(splits[5], part), 71), part)
    ln_gain = jnp.clip(1.0 + 0.18 * jax.random.normal(splits[1], (D,), jnp.float32), 0.1, 1.9)
    w_qkv = draw_w_qkv(jax.random.fold_in(splits[5], 71), part)
    qk_gains = draw_qk_gains(jax.random.fold_in(splits[5], 71), part)
    w_out = scatter_about(splits[4], (D, D), D ** -0.5, 0.1875)
    return {"patches": patches, "ln_gain": ln_gain, "w_qkv": w_qkv, "qk_gains": qk_gains, "w_out": w_out}


def layer_norm(patches, ln_gain):
    values_f = patches.astype(jnp.float32)
    centre = values_f - lax.optimization_barrier(jnp.mean(values_f, axis=-1, keepdims=True))
    variance = lax.optimization_barrier(jnp.mean(centre * centre, axis=-1, keepdims=True))
    return (centre * lax.rsqrt(variance + 1e-05) * ln_gain).astype(jnp.bfloat16)

def head_norm(columns, gain_vector, head_count):
    row_count = columns.shape[0]
    shaped = columns.reshape(row_count, head_count, HD)
    square_mean = lax.optimization_barrier(jnp.mean(shaped * shaped, axis=-1, keepdims=True))
    scaled = shaped * lax.rsqrt(square_mean + 1e-06) * gain_vector.reshape(head_count, HD)
    return scaled.astype(jnp.bfloat16).reshape(row_count, head_count * HD)

def reference(patches, ln_gain, w_qkv, qk_gains, w_out):
    normed = layer_norm(patches, ln_gain)
    projected = jnp.dot(normed, w_qkv, preferred_element_type=jnp.float32)
    query = head_norm(projected[:, :D], qk_gains[0], H)
    key_rows = head_norm(projected[:, D:2 * D], qk_gains[1], H)
    value_rows = projected[:, 2 * D:].astype(jnp.bfloat16)
    seq_count = patches.shape[0]
    block_rows = 512 if seq_count % 512 == 0 else seq_count
    score_scale = HD ** (-0.5)

    def one_head(triple):
        query_head, key_head, value_head = triple
        query_blocks = query_head.reshape(seq_count // block_rows, block_rows, HD)

        def one_block(query_block):
            scores = jnp.dot(query_block, key_head.T, preferred_element_type=jnp.float32) * score_scale
            row_max = lax.optimization_barrier(jnp.max(scores, axis=-1, keepdims=True))
            exponent = jnp.exp(scores - row_max)
            totals = lax.optimization_barrier(jnp.sum(exponent, axis=-1, keepdims=True))
            summed = jnp.dot(exponent.astype(jnp.bfloat16), value_head, preferred_element_type=jnp.float32)
            return (summed / totals).astype(jnp.bfloat16)
        return lax.map(one_block, query_blocks).reshape(seq_count, HD)

    def by_head(rows_matrix):
        return jnp.transpose(rows_matrix.reshape(seq_count, H, HD), (1, 0, 2))
    attended = lax.map(one_head, (by_head(query), by_head(key_rows), by_head(value_rows)))
    attended = jnp.transpose(attended, (1, 0, 2)).reshape(seq_count, D)
    return jnp.dot(attended, w_out, preferred_element_type=jnp.float32).astype(jnp.bfloat16)
```

```python
import functools

import jax
import jax.numpy as jnp
from jax import lax
from jax.experimental import pallas as pl
from jax.experimental.pallas import tpu as pltpu
from jax.sharding import PartitionSpec as P

H = 16
HD = 64
F32 = jnp.float32
BF16 = jnp.bfloat16


def dot(a, b):
    return jnp.dot(a, b, preferred_element_type=F32)


def dot_nt(a, b):
    return lax.dot_general(a, b, (((1,), (1,)), ((), ())), preferred_element_type=F32)


def kernel(
    n, rows, width,
    patches, ln_gain, gains, w_qkv, w_out, out,
    xg, wq, wk, wv, wvt, wo, qbd, ones, m_ref, l_ref, acc, att, att_in,
    w_sem, ring_send, ring_recv, sib_send, sib_recv, att_send, att_recv,
):
    d = patches.shape[1]
    nq = 2 * rows
    half = rows // 2
    pairs = width // (2 * HD)
    g, c, b = lax.axis_index("group"), lax.axis_index("head"), lax.axis_index("blk")
    odd = b % 2
    up = jnp.where(b == n - 2, n - 1, b + 2)
    down = jnp.where(b == 1, 0, b - 2)
    nxt = jnp.where(odd == 1, down, up)
    up_p = jnp.where(b == n - 1, n - 2, b + 2)
    down_p = jnp.where(b == 0, 1, b - 2)
    prv = jnp.where(odd == 1, up_p, down_p)
    towards = ((g, c, nxt), (g, c, prv))
    sibling = (g, 1 - c, b)

    barrier = pltpu.get_barrier_semaphore()
    for peer in (*towards, sibling):
        pl.semaphore_signal(barrier, inc=1, device_id=peer, device_id_type=pl.DeviceIdType.MESH)

    def fetch(part, target):
        columns = pl.ds(pl.multiple_of(part * d + c * width, 128), width)
        return pltpu.make_async_copy(w_qkv.at[:, columns], target, w_sem.at[part])

    loads = [fetch(0, wq), fetch(1, wk), fetch(2, wv)]
    for load in loads:
        load.start()
    load_out = pltpu.make_async_copy(w_out, wo, w_sem.at[3])
    load_out.start()

    mine = pl.ds(pl.multiple_of(c * rows, rows), rows)
    theirs = pl.ds(pl.multiple_of((1 - c) * rows, rows), rows)

    def piece(k, which):
        return xg.at[k, pl.ds(pl.multiple_of(c * rows + which * half, half), half), :]

    def hop(way, k, source):
        return pltpu.make_async_remote_copy(
            src_ref=source,
            dst_ref=piece(k, way),
            send_sem=ring_send.at[way, k],
            recv_sem=ring_recv.at[way, k],
            device_id=towards[way],
            device_id_type=pl.DeviceIdType.MESH,
        )

    def across(k):
        return pltpu.make_async_remote_copy(
            src_ref=xg.at[k, mine, :],
            dst_ref=xg.at[k, mine, :],
            send_sem=sib_send.at[k],
            recv_sem=sib_recv.at[k],
            device_id=sibling,
            device_id_type=pl.DeviceIdType.MESH,
        )

    def across_in(k):
        return pltpu.make_async_remote_copy(
            src_ref=xg.at[k, theirs, :],
            dst_ref=xg.at[k, theirs, :],
            send_sem=sib_send.at[k],
            recv_sem=sib_recv.at[k],
            device_id=sibling,
            device_id_type=pl.DeviceIdType.MESH,
        )

    x = patches[...].astype(F32)
    centre = x - jnp.mean(x, axis=-1, keepdims=True)
    variance = jnp.mean(centre * centre, axis=-1, keepdims=True)
    xg[0, mine, :] = (centre * lax.rsqrt(variance + 1e-05) * ln_gain[...]).astype(BF16)

    pl.semaphore_wait(barrier, 3)
    across(0).start()
    for h in range(2):
        for way in range(2):
            hop(way, 1 + h, piece(0, h)).start()

    row_id = lax.broadcasted_iota(jnp.int32, (4 * HD, 4 * HD), 0) >> 6
    col_id = lax.broadcasted_iota(jnp.int32, (4 * HD, 4 * HD), 1) >> 6
    ones[...] = jnp.where(row_id == col_id, 1.0, 0.0).astype(BF16)
    m_ref[...] = jnp.full(m_ref.shape, -1e30, F32)
    l_ref[...] = jnp.zeros(l_ref.shape, F32)
    acc[...] = jnp.zeros(acc.shape, F32)
    qbd[...] = jnp.zeros(qbd.shape, BF16)

    def head_norm(columns, gain):
        parts = []
        for i in range(width // (4 * HD)):
            block = columns[:, i * 4 * HD : (i + 1) * 4 * HD]
            total = dot((block * block).astype(BF16), ones[...])
            parts.append(block * lax.rsqrt(total * (1.0 / HD) + 1e-06))
        return jnp.concatenate(parts, axis=1) * gain

    gain_columns = pl.ds(pl.multiple_of(c * width, 128), width)
    gain_q = gains[0:1, gain_columns]
    gain_k = gains[1:2, gain_columns]

    loads[2].wait()
    wvt[...] = wv[...].T
    loads[0].wait()
    across_in(0).wait_recv()
    query = head_norm(dot(xg[0], wq[...]), gain_q).astype(BF16).astype(F32) * (HD ** -0.5)
    for j in range(pairs):
        block = query[:, j * 2 * HD : (j + 1) * 2 * HD].T.astype(BF16)
        qbd[j, 0:HD, 0:nq] = block[0:HD]
        qbd[j, HD : 2 * HD, nq : 2 * nq] = block[HD : 2 * HD]
    loads[1].wait()

    def absorb(k):
        tokens = xg[k]
        keys = head_norm(dot(tokens, wk[...]), gain_k).astype(BF16)
        values_t = dot_nt(wvt[...], tokens).astype(BF16)
        for j in range(pairs):
            scores = dot(keys[:, j * 2 * HD : (j + 1) * 2 * HD], qbd[j])
            old = m_ref[j]
            new = jnp.maximum(old, jnp.max(scores, axis=0, keepdims=True))
            shrink = jnp.exp(old - new)
            weights = jnp.exp(scores - new)
            m_ref[j] = new
            l_ref[j] = l_ref[j] * shrink + jnp.sum(weights, axis=0, keepdims=True)
            weights = weights.astype(BF16)
            for e in range(2):
                channels = slice((2 * j + e) * HD, (2 * j + e + 1) * HD)
                span = slice(e * nq, (e + 1) * nq)
                acc[channels, :] = acc[channels, :] * shrink[:, span] + dot(
                    values_t[channels], weights[:, span]
                )

    absorb(0)

    def step(k, carry):
        for way in range(2):
            hop(way, k, piece(k, way)).wait_recv()

            @pl.when(k < n - 3)
            def _():
                hop(way, k + 2, piece(k, way)).start()

            @pl.when(k == n - 3 + way)
            def _():
                hop(way, n - 1, piece(k, way)).start()

        across(k).start()

        @pl.when(k >= 2)
        def _():
            across_in(k - 1).wait_recv()
            absorb(k - 1)

        return carry

    lax.fori_loop(1, n, step, 0)
    across_in(n - 1).wait_recv()
    absorb(n - 1)

    for j in range(pairs):
        inverse = 1.0 / l_ref[j]
        for e in range(2):
            channels = slice((2 * j + e) * HD, (2 * j + e + 1) * HD)
            acc[channels, :] = acc[channels, :] * inverse[:, e * nq : (e + 1) * nq]
        both = slice(2 * j * HD, 2 * (j + 1) * HD)
        att[:, both] = acc[both, :].T.astype(BF16)
    swap = pltpu.make_async_remote_copy(
        src_ref=att.at[theirs, :],
        dst_ref=att_in,
        send_sem=att_send,
        recv_sem=att_recv,
        device_id=sibling,
        device_id_type=pl.DeviceIdType.MESH,
    )
    swap.start()
    load_out.wait()
    my_heads = pl.ds(pl.multiple_of(c * width, width), width)
    their_heads = pl.ds(pl.multiple_of((1 - c) * width, width), width)
    partial = dot(att[mine, :], wo[my_heads, :])
    swap.wait_recv()
    out[...] = (partial + dot(att_in[...], wo[their_heads, :])).astype(BF16)

    swap.wait_send()
    across(0).wait_send()

    def drain(k, carry):
        for way in range(2):
            hop(way, k, piece(k, way)).wait_send()
        across(k).wait_send()
        return carry

    lax.fori_loop(1, n, drain, 0)


def per_device(patches, ln_gain, w_qkv, qk_gains, w_out):
    rows, d = patches.shape
    n = lax.axis_size("blk")
    width = H // lax.axis_size("head") * HD
    nq = 2 * rows
    vmem = pl.BlockSpec(memory_space=pltpu.VMEM)
    hbm = pl.BlockSpec(memory_space=pl.ANY)
    return pl.pallas_call(
        functools.partial(kernel, n, rows, width),
        out_shape=jax.ShapeDtypeStruct((rows, d), BF16),
        in_specs=[vmem, vmem, vmem, hbm, hbm],
        out_specs=vmem,
        scratch_shapes=[
            pltpu.VMEM((n, nq, d), BF16),
            pltpu.VMEM((d, width), BF16),
            pltpu.VMEM((d, width), BF16),
            pltpu.VMEM((d, width), BF16),
            pltpu.VMEM((width, d), BF16),
            pltpu.VMEM((d, d), BF16),
            pltpu.VMEM((width // (2 * HD), 2 * HD, 2 * nq), BF16),
            pltpu.VMEM((4 * HD, 4 * HD), BF16),
            pltpu.VMEM((width // (2 * HD), 1, 2 * nq), F32),
            pltpu.VMEM((width // (2 * HD), 1, 2 * nq), F32),
            pltpu.VMEM((width, nq), F32),
            pltpu.VMEM((nq, width), BF16),
            pltpu.VMEM((rows, width), BF16),
            pltpu.SemaphoreType.DMA((4,)),
            pltpu.SemaphoreType.DMA((2, n)),
            pltpu.SemaphoreType.DMA((2, n)),
            pltpu.SemaphoreType.DMA((n,)),
            pltpu.SemaphoreType.DMA((n,)),
            pltpu.SemaphoreType.DMA,
            pltpu.SemaphoreType.DMA,
        ],
        compiler_params=pltpu.CompilerParams(
            collective_id=0, has_side_effects=True, vmem_limit_bytes=48 << 20
        ),
    )(patches, ln_gain.reshape(1, d), qk_gains, w_qkv, w_out)


def solution(mesh):
    placed = (P(("group", "head", "blk"), None), P(), P(), P(), P())
    return jax.shard_map(
        per_device,
        mesh=mesh,
        in_specs=placed,
        out_specs=P(("group", "head", "blk"), None),
        check_vma=False,
    )
```

```python
import functools

import jax
import jax.numpy as jnp
from jax import lax
from jax.experimental import pallas as pl
from jax.experimental.pallas import tpu as pltpu
from jax.sharding import PartitionSpec as P

H = 16
HD = 64
F32 = jnp.float32
BF16 = jnp.bfloat16


def dot(a, b):
    return jnp.dot(a, b, preferred_element_type=F32)


def dot_nt(a, b):
    return lax.dot_general(a, b, (((1,), (1,)), ((), ())), preferred_element_type=F32)


def kernel(
    n, rows, width,
    patches_hbm, ln_gain_hbm, gains_hbm, w_qkv, w_out, out,
    patches, ln_gain, gains, xg, wq, wk, wv, wvt, wo, qbd, ones, m_ref, l_ref, acc, att, att_in,
    w_sem, ring_send, ring_recv, sib_send, sib_recv, att_send, att_recv,
):
    d = patches_hbm.shape[1]
    nq = 2 * rows
    half = rows // 2
    pairs = width // (2 * HD)
    g, c, b = lax.axis_index("group"), lax.axis_index("head"), lax.axis_index("blk")
    odd = b % 2
    up = jnp.where(b == n - 2, n - 1, b + 2)
    down = jnp.where(b == 1, 0, b - 2)
    nxt = jnp.where(odd == 1, down, up)
    up_p = jnp.where(b == n - 1, n - 2, b + 2)
    down_p = jnp.where(b == 0, 1, b - 2)
    prv = jnp.where(odd == 1, up_p, down_p)
    towards = ((g, c, nxt), (g, c, prv))
    sibling = (g, 1 - c, b)

    small = [
        pltpu.make_async_copy(source, target, w_sem.at[4 + i])
        for i, (source, target) in enumerate(
            ((patches_hbm, patches), (ln_gain_hbm, ln_gain), (gains_hbm, gains))
        )
    ]
    for load in small:
        load.start()
    barrier = pltpu.get_barrier_semaphore()
    for peer in (*towards, sibling):
        pl.semaphore_signal(barrier, inc=1, device_id=peer, device_id_type=pl.DeviceIdType.MESH)

    def fetch(part, target):
        columns = pl.ds(pl.multiple_of(part * d + c * width, 128), width)
        return pltpu.make_async_copy(w_qkv.at[:, columns], target, w_sem.at[part])

    loads = [fetch(0, wq), fetch(1, wk), fetch(2, wv)]
    for load in loads:
        load.start()
    load_out = pltpu.make_async_copy(w_out, wo, w_sem.at[3])
    load_out.start()

    mine = pl.ds(pl.multiple_of(c * rows, rows), rows)
    theirs = pl.ds(pl.multiple_of((1 - c) * rows, rows), rows)

    def piece(k, which):
        return xg.at[k, pl.ds(pl.multiple_of(c * rows + which * half, half), half), :]

    def hop(way, k, source):
        return pltpu.make_async_remote_copy(
            src_ref=source,
            dst_ref=piece(k, way),
            send_sem=ring_send.at[way, k],
            recv_sem=ring_recv.at[way, k],
            device_id=towards[way],
            device_id_type=pl.DeviceIdType.MESH,
        )

    def across(k):
        return pltpu.make_async_remote_copy(
            src_ref=xg.at[k, mine, :],
            dst_ref=xg.at[k, mine, :],
            send_sem=sib_send.at[k],
            recv_sem=sib_recv.at[k],
            device_id=sibling,
            device_id_type=pl.DeviceIdType.MESH,
        )

    def across_in(k):
        return pltpu.make_async_remote_copy(
            src_ref=xg.at[k, theirs, :],
            dst_ref=xg.at[k, theirs, :],
            send_sem=sib_send.at[k],
            recv_sem=sib_recv.at[k],
            device_id=sibling,
            device_id_type=pl.DeviceIdType.MESH,
        )

    small[0].wait()
    small[1].wait()
    x = patches[...].astype(F32)
    centre = x - jnp.mean(x, axis=-1, keepdims=True)
    variance = jnp.mean(centre * centre, axis=-1, keepdims=True)
    xg[0, mine, :] = (centre * lax.rsqrt(variance + 1e-05) * ln_gain[...]).astype(BF16)

    pl.semaphore_wait(barrier, 3)
    across(0).start()
    for h in range(2):
        for way in range(2):
            hop(way, 1 + h, piece(0, h)).start()

    row_id = lax.broadcasted_iota(jnp.int32, (4 * HD, 4 * HD), 0) >> 6
    col_id = lax.broadcasted_iota(jnp.int32, (4 * HD, 4 * HD), 1) >> 6
    ones[...] = jnp.where(row_id == col_id, 1.0, 0.0).astype(BF16)
    m_ref[...] = jnp.full(m_ref.shape, -1e30, F32)
    l_ref[...] = jnp.zeros(l_ref.shape, F32)
    acc[...] = jnp.zeros(acc.shape, F32)
    qbd[...] = jnp.zeros(qbd.shape, BF16)

    def head_norm(columns, gain):
        parts = []
        for i in range(width // (4 * HD)):
            block = columns[:, i * 4 * HD : (i + 1) * 4 * HD]
            total = dot((block * block).astype(BF16), ones[...])
            parts.append(block * lax.rsqrt(total * (1.0 / HD) + 1e-06))
        return jnp.concatenate(parts, axis=1) * gain

    gain_columns = pl.ds(pl.multiple_of(c * width, 128), width)
    small[2].wait()
    gain_q = gains[0:1, gain_columns]
    gain_k = gains[1:2, gain_columns]

    loads[2].wait()
    wvt[...] = wv[...].T
    loads[0].wait()
    across_in(0).wait_recv()
    query = head_norm(dot(xg[0], wq[...]), gain_q).astype(BF16).astype(F32) * (HD ** -0.5)
    for j in range(pairs):
        block = query[:, j * 2 * HD : (j + 1) * 2 * HD].T.astype(BF16)
        qbd[j, 0:HD, 0:nq] = block[0:HD]
        qbd[j, HD : 2 * HD, nq : 2 * nq] = block[HD : 2 * HD]
    loads[1].wait()

    def absorb(k):
        tokens = xg[k]
        keys = head_norm(dot(tokens, wk[...]), gain_k).astype(BF16)
        values_t = dot_nt(wvt[...], tokens).astype(BF16)
        for j in range(pairs):
            scores = dot(keys[:, j * 2 * HD : (j + 1) * 2 * HD], qbd[j])
            old = m_ref[j]
            new = jnp.maximum(old, jnp.max(scores, axis=0, keepdims=True))
            shrink = jnp.exp(old - new)
            weights = jnp.exp(scores - new)
            m_ref[j] = new
            l_ref[j] = l_ref[j] * shrink + jnp.sum(weights, axis=0, keepdims=True)
            weights = weights.astype(BF16)
            for e in range(2):
                channels = slice((2 * j + e) * HD, (2 * j + e + 1) * HD)
                span = slice(e * nq, (e + 1) * nq)
                acc[channels, :] = acc[channels, :] * shrink[:, span] + dot(
                    values_t[channels], weights[:, span]
                )

    def receive(k):
        for way in range(2):
            hop(way, k, piece(k, way)).wait_recv()

            @pl.when(k < n - 3)
            def _():
                hop(way, k + 2, piece(k, way)).start()

            @pl.when(k == n - 3 + way)
            def _():
                hop(way, n - 1, piece(k, way)).start()

        across(k).start()

    def step(k, carry):
        @pl.when(k < n - 1)
        def _():
            receive(k)

        @pl.when(k >= 2)
        def _():
            across_in(k - 1).wait_recv()

        absorb(k - 1)

        @pl.when(k == n - 1)
        def _():
            receive(k)

        return carry

    lax.fori_loop(1, n + 1, step, 0)

    for j in range(pairs):
        inverse = 1.0 / l_ref[j]
        for e in range(2):
            channels = slice((2 * j + e) * HD, (2 * j + e + 1) * HD)
            acc[channels, :] = acc[channels, :] * inverse[:, e * nq : (e + 1) * nq]
        both = slice(2 * j * HD, 2 * (j + 1) * HD)
        att[:, both] = acc[both, :].T.astype(BF16)
    swap = pltpu.make_async_remote_copy(
        src_ref=att.at[theirs, :],
        dst_ref=att_in,
        send_sem=att_send,
        recv_sem=att_recv,
        device_id=sibling,
        device_id_type=pl.DeviceIdType.MESH,
    )
    swap.start()
    load_out.wait()
    my_heads = pl.ds(pl.multiple_of(c * width, width), width)
    their_heads = pl.ds(pl.multiple_of((1 - c) * width, width), width)
    partial = dot(att[mine, :], wo[my_heads, :])
    swap.wait_recv()
    out[...] = (partial + dot(att_in[...], wo[their_heads, :])).astype(BF16)

    swap.wait_send()
    across(0).wait_send()

    def drain(k, carry):
        for way in range(2):
            hop(way, k, piece(k, way)).wait_send()
        across(k).wait_send()
        return carry

    lax.fori_loop(1, n, drain, 0)


def per_device(patches, ln_gain, w_qkv, qk_gains, w_out):
    rows, d = patches.shape
    n = lax.axis_size("blk")
    width = H // lax.axis_size("head") * HD
    nq = 2 * rows
    vmem = pl.BlockSpec(memory_space=pltpu.VMEM)
    hbm = pl.BlockSpec(memory_space=pltpu.HBM)
    return pl.pallas_call(
        functools.partial(kernel, n, rows, width),
        out_shape=jax.ShapeDtypeStruct((rows, d), BF16),
        in_specs=[hbm, hbm, hbm, hbm, hbm],
        out_specs=vmem,
        scratch_shapes=[
            pltpu.VMEM((rows, d), BF16),
            pltpu.VMEM((1, d), F32),
            pltpu.VMEM((2, d), F32),
            pltpu.VMEM((n, nq, d), BF16),
            pltpu.VMEM((d, width), BF16),
            pltpu.VMEM((d, width), BF16),
            pltpu.VMEM((d, width), BF16),
            pltpu.VMEM((width, d), BF16),
            pltpu.VMEM((d, d), BF16),
            pltpu.VMEM((width // (2 * HD), 2 * HD, 2 * nq), BF16),
            pltpu.VMEM((4 * HD, 4 * HD), BF16),
            pltpu.VMEM((width // (2 * HD), 1, 2 * nq), F32),
            pltpu.VMEM((width // (2 * HD), 1, 2 * nq), F32),
            pltpu.VMEM((width, nq), F32),
            pltpu.VMEM((nq, width), BF16),
            pltpu.VMEM((rows, width), BF16),
            pltpu.SemaphoreType.DMA((7,)),
            pltpu.SemaphoreType.DMA((2, n)),
            pltpu.SemaphoreType.DMA((2, n)),
            pltpu.SemaphoreType.DMA((n,)),
            pltpu.SemaphoreType.DMA((n,)),
            pltpu.SemaphoreType.DMA,
            pltpu.SemaphoreType.DMA,
        ],
        compiler_params=pltpu.CompilerParams(
            collective_id=0, has_side_effects=True, vmem_limit_bytes=56 << 20
        ),
    )(patches, ln_gain.reshape(1, d), qk_gains, w_qkv, w_out)


def solution(mesh):
    placed = (P(("group", "head", "blk"), None), P(), P(), P(), P())
    return jax.shard_map(
        per_device,
        mesh=mesh,
        in_specs=placed,
        out_specs=P(("group", "head", "blk"), None),
        check_vma=False,
    )
```

```python
import functools

import jax
import jax.numpy as jnp
from jax import lax
from jax.experimental import pallas as pl
from jax.experimental.pallas import tpu as pltpu
from jax.sharding import PartitionSpec as P

H = 16
HD = 64
PARTS = 2
F32 = jnp.float32
BF16 = jnp.bfloat16


def dot(a, b):
    return jnp.dot(a, b, preferred_element_type=F32)


def dot_nt(a, b):
    return lax.dot_general(a, b, (((1,), (1,)), ((), ())), preferred_element_type=F32)


def kernel(
    n, rows, width,
    patches_hbm, ln_gain_hbm, gains_hbm, w_qkv, w_out, out,
    patches, ln_gain, gains, xg, wq, wk, wv, wvt, wo, qbd, ones, m_ref, l_ref, acc, att, att_in,
    w_sem, ring_send, ring_recv, sib_send, sib_recv, att_send, att_recv,
):
    d = patches_hbm.shape[1]
    nq = 2 * rows
    half = rows // 2
    sub = half // PARTS
    pairs = width // (2 * HD)
    g, c, b = lax.axis_index("group"), lax.axis_index("head"), lax.axis_index("blk")
    odd = b % 2
    up = jnp.where(b == n - 2, n - 1, b + 2)
    down = jnp.where(b == 1, 0, b - 2)
    nxt = jnp.where(odd == 1, down, up)
    up_p = jnp.where(b == n - 1, n - 2, b + 2)
    down_p = jnp.where(b == 0, 1, b - 2)
    prv = jnp.where(odd == 1, up_p, down_p)
    towards = ((g, c, nxt), (g, c, prv))
    sibling = (g, 1 - c, b)

    small = [
        pltpu.make_async_copy(source, target, w_sem.at[4 + i])
        for i, (source, target) in enumerate(
            ((patches_hbm, patches), (ln_gain_hbm, ln_gain), (gains_hbm, gains))
        )
    ]
    for load in small:
        load.start()
    barrier = pltpu.get_barrier_semaphore()
    for peer in (*towards, sibling):
        pl.semaphore_signal(barrier, inc=1, device_id=peer, device_id_type=pl.DeviceIdType.MESH)

    def fetch(part, target):
        columns = pl.ds(pl.multiple_of(part * d + c * width, 128), width)
        return pltpu.make_async_copy(w_qkv.at[:, columns], target, w_sem.at[part])

    loads = [fetch(0, wq), fetch(1, wk), fetch(2, wv)]
    for load in loads:
        load.start()
    load_out = pltpu.make_async_copy(w_out, wo, w_sem.at[3])
    load_out.start()

    mine = pl.ds(pl.multiple_of(c * rows, rows), rows)
    theirs = pl.ds(pl.multiple_of((1 - c) * rows, rows), rows)

    def piece(k, which, part):
        first = pl.multiple_of(c * rows + which * half + part * sub, sub)
        return xg.at[k, pl.ds(first, sub), :]

    def hop(way, k, part, source):
        return pltpu.make_async_remote_copy(
            src_ref=source,
            dst_ref=piece(k, way, part),
            send_sem=ring_send.at[way, k, part],
            recv_sem=ring_recv.at[way, k, part],
            device_id=towards[way],
            device_id_type=pl.DeviceIdType.MESH,
        )

    def across(k):
        return pltpu.make_async_remote_copy(
            src_ref=xg.at[k, mine, :],
            dst_ref=xg.at[k, mine, :],
            send_sem=sib_send.at[k],
            recv_sem=sib_recv.at[k],
            device_id=sibling,
            device_id_type=pl.DeviceIdType.MESH,
        )

    def across_in(k):
        return pltpu.make_async_remote_copy(
            src_ref=xg.at[k, theirs, :],
            dst_ref=xg.at[k, theirs, :],
            send_sem=sib_send.at[k],
            recv_sem=sib_recv.at[k],
            device_id=sibling,
            device_id_type=pl.DeviceIdType.MESH,
        )

    small[0].wait()
    small[1].wait()
    x = patches[...].astype(F32)
    centre = x - jnp.mean(x, axis=-1, keepdims=True)
    variance = jnp.mean(centre * centre, axis=-1, keepdims=True)
    xg[0, mine, :] = (centre * lax.rsqrt(variance + 1e-05) * ln_gain[...]).astype(BF16)

    pl.semaphore_wait(barrier, 3)
    across(0).start()
    for h in range(2):
        for part in range(PARTS):
            for way in range(2):
                hop(way, 1 + h, part, piece(0, h, part)).start()

    row_id = lax.broadcasted_iota(jnp.int32, (4 * HD, 4 * HD), 0) >> 6
    col_id = lax.broadcasted_iota(jnp.int32, (4 * HD, 4 * HD), 1) >> 6
    ones[...] = jnp.where(row_id == col_id, 1.0, 0.0).astype(BF16)
    m_ref[...] = jnp.full(m_ref.shape, -1e30, F32)
    l_ref[...] = jnp.zeros(l_ref.shape, F32)
    acc[...] = jnp.zeros(acc.shape, F32)
    qbd[...] = jnp.zeros(qbd.shape, BF16)

    def head_norm(columns, gain):
        parts = []
        for i in range(width // (4 * HD)):
            block = columns[:, i * 4 * HD : (i + 1) * 4 * HD]
            total = dot((block * block).astype(BF16), ones[...])
            parts.append(block * lax.rsqrt(total * (1.0 / HD) + 1e-06))
        return jnp.concatenate(parts, axis=1) * gain

    gain_columns = pl.ds(pl.multiple_of(c * width, 128), width)
    small[2].wait()
    gain_q = gains[0:1, gain_columns]
    gain_k = gains[1:2, gain_columns]

    loads[2].wait()
    wvt[...] = wv[...].T
    loads[0].wait()
    across_in(0).wait_recv()
    query = head_norm(dot(xg[0], wq[...]), gain_q).astype(BF16).astype(F32) * (HD ** -0.5)
    for j in range(pairs):
        block = query[:, j * 2 * HD : (j + 1) * 2 * HD].T.astype(BF16)
        qbd[j, 0:HD, 0:nq] = block[0:HD]
        qbd[j, HD : 2 * HD, nq : 2 * nq] = block[HD : 2 * HD]
    loads[1].wait()

    def absorb_rows(tokens):
        keys = head_norm(dot(tokens, wk[...]), gain_k).astype(BF16)
        values_t = dot_nt(wvt[...], tokens).astype(BF16)
        for j in range(pairs):
            scores = dot(keys[:, j * 2 * HD : (j + 1) * 2 * HD], qbd[j])
            old = m_ref[j]
            new = jnp.maximum(old, jnp.max(scores, axis=0, keepdims=True))
            shrink = jnp.exp(old - new)
            weights = jnp.exp(scores - new)
            m_ref[j] = new
            l_ref[j] = l_ref[j] * shrink + jnp.sum(weights, axis=0, keepdims=True)
            weights = weights.astype(BF16)
            for e in range(2):
                channels = slice((2 * j + e) * HD, (2 * j + e + 1) * HD)
                span = slice(e * nq, (e + 1) * nq)
                acc[channels, :] = acc[channels, :] * shrink[:, span] + dot(
                    values_t[channels], weights[:, span]
                )

    def absorb(k):
        absorb_rows(xg[k])

    def receive(k):
        for part in range(PARTS):
            for way in range(2):
                hop(way, k, part, piece(k, way, part)).wait_recv()

                @pl.when(k < n - 3)
                def _():
                    hop(way, k + 2, part, piece(k, way, part)).start()

                @pl.when(k == n - 3 + way)
                def _():
                    hop(way, n - 1, part, piece(k, way, part)).start()

        across(k).start()

    def step(k, carry):
        @pl.when((k >= 2) & (k < n - 1))
        def _():
            receive(k)

        @pl.when(k >= 2)
        def _():
            across_in(k - 1).wait_recv()

        absorb(k - 1)

        @pl.when((k == 1) | (k == n - 1))
        def _():
            receive(k)

        return carry

    lax.fori_loop(1, n, step, 0)

    def last(i, carry):
        @pl.when(i == 1)
        def _():
            across_in(n - 1).wait_recv()

        first = (c + i - 2 * c * i) * rows
        absorb_rows(xg[n - 1, pl.ds(pl.multiple_of(first, rows), rows), :])
        return carry

    lax.fori_loop(0, 2, last, 0)

    for j in range(pairs):
        inverse = 1.0 / l_ref[j]
        for e in range(2):
            channels = slice((2 * j + e) * HD, (2 * j + e + 1) * HD)
            acc[channels, :] = acc[channels, :] * inverse[:, e * nq : (e + 1) * nq]
        both = slice(2 * j * HD, 2 * (j + 1) * HD)
        att[:, both] = acc[both, :].T.astype(BF16)
    swap = pltpu.make_async_remote_copy(
        src_ref=att.at[theirs, :],
        dst_ref=att_in,
        send_sem=att_send,
        recv_sem=att_recv,
        device_id=sibling,
        device_id_type=pl.DeviceIdType.MESH,
    )
    swap.start()
    load_out.wait()
    my_heads = pl.ds(pl.multiple_of(c * width, width), width)
    their_heads = pl.ds(pl.multiple_of((1 - c) * width, width), width)
    partial = dot(att[mine, :], wo[my_heads, :])
    swap.wait_recv()
    out[...] = (partial + dot(att_in[...], wo[their_heads, :])).astype(BF16)

    swap.wait_send()
    across(0).wait_send()

    def drain(k, carry):
        for part in range(PARTS):
            for way in range(2):
                hop(way, k, part, piece(k, way, part)).wait_send()
        across(k).wait_send()
        return carry

    lax.fori_loop(1, n, drain, 0)


def per_device(patches, ln_gain, w_qkv, qk_gains, w_out):
    rows, d = patches.shape
    n = lax.axis_size("blk")
    width = H // lax.axis_size("head") * HD
    nq = 2 * rows
    vmem = pl.BlockSpec(memory_space=pltpu.VMEM)
    hbm = pl.BlockSpec(memory_space=pltpu.HBM)
    return pl.pallas_call(
        functools.partial(kernel, n, rows, width),
        out_shape=jax.ShapeDtypeStruct((rows, d), BF16),
        in_specs=[hbm, hbm, hbm, hbm, hbm],
        out_specs=vmem,
        scratch_shapes=[
            pltpu.VMEM((rows, d), BF16),
            pltpu.VMEM((1, d), F32),
            pltpu.VMEM((2, d), F32),
            pltpu.VMEM((n, nq, d), BF16),
            pltpu.VMEM((d, width), BF16),
            pltpu.VMEM((d, width), BF16),
            pltpu.VMEM((d, width), BF16),
            pltpu.VMEM((width, d), BF16),
            pltpu.VMEM((d, d), BF16),
            pltpu.VMEM((width // (2 * HD), 2 * HD, 2 * nq), BF16),
            pltpu.VMEM((4 * HD, 4 * HD), BF16),
            pltpu.VMEM((width // (2 * HD), 1, 2 * nq), F32),
            pltpu.VMEM((width // (2 * HD), 1, 2 * nq), F32),
            pltpu.VMEM((width, nq), F32),
            pltpu.VMEM((nq, width), BF16),
            pltpu.VMEM((rows, width), BF16),
            pltpu.SemaphoreType.DMA((7,)),
            pltpu.SemaphoreType.DMA((2, n, PARTS)),
            pltpu.SemaphoreType.DMA((2, n, PARTS)),
            pltpu.SemaphoreType.DMA((n,)),
            pltpu.SemaphoreType.DMA((n,)),
            pltpu.SemaphoreType.DMA,
            pltpu.SemaphoreType.DMA,
        ],
        compiler_params=pltpu.CompilerParams(
            collective_id=0, has_side_effects=True, vmem_limit_bytes=56 << 20
        ),
    )(patches, ln_gain.reshape(1, d), qk_gains, w_qkv, w_out)


def solution(mesh):
    placed = (P(("group", "head", "blk"), None), P(), P(), P(), P())
    return jax.shard_map(
        per_device,
        mesh=mesh,
        in_specs=placed,
        out_specs=P(("group", "head", "blk"), None),
        check_vma=False,
    )
```
